512 devices in a mesh: ta: 4 (over z_hi), ha: 8 (over x, core), wa: 16 (over y, z_lo).
Axes of the slice: x: 4, y: 8, z: 8 (z_hi: 4, z_lo: 2; z = z_hi * 2 + z_lo), core: 2. Of those that a mesh axis runs over, the one named last changes fastest.
Arguments:
- query_in: bfloat16 [12, 64, 128, 256], P('ta', 'ha', 'wa'), may hold values from -24 to 24
- key_in: bfloat16 [12, 64, 128, 256], P('ta', 'ha', 'wa'), may hold values from -24 to 24
- value_in: bfloat16 [12, 64, 128, 256], P('ta', 'ha', 'wa'), may hold values from -6 to 6
- cotangent: bfloat16 [12, 64, 128, 256], P('ta', 'ha', 'wa'), may hold values from -6 to 6
Outputs:
- attended: bfloat16 [12, 64, 128, 256], P('ta', 'ha', 'wa')
- grad_query: bfloat16 [12, 64, 128, 256], P('ta', 'ha', 'wa')
- grad_key: bfloat16 [12, 64, 128, 256], P('ta', 'ha', 'wa')
- grad_value: bfloat16 [12, 64, 128, 256], P('ta', 'ha', 'wa')
The draws below stay inside these ranges and needn't reach their ends.
All inputs are finite; a program needn't handle non-finite values.
Results may differ from the reference program's by a relative error of at most 0.035.
Values may be sent and summed in bfloat16 or wider, within the bound.
A program may use at most 128 MiB of HBM per device.

```python
import jax
import jax.numpy as jnp
from jax import lax

DH = 128
HEADS = 2
TILE_T = 6
TILE_H = 8
TILE_W = 8
NT = 12
NH = 64
NW = 128


def drawn_pair(key):
    shape_all = (NT, NH, NW, HEADS * DH)
    query_base = jnp.clip(jax.random.normal(jax.random.fold_in(key, 11), shape_all, jnp.float32), -6.0, 6.0)
    key_base = jnp.clip(jax.random.normal(jax.random.fold_in(key, 12), shape_all, jnp.float32), -6.0, 6.0)
    return (query_base, key_base)


def draw_query_in(key, part):
    return drawn_pair(key)[0].astype(jnp.bfloat16)


def draw_key_in(key, part):
    return drawn_pair(key)[1].astype(jnp.bfloat16)


def block_levels(rng, dims, pieces, low, top_value):
    loudness = 1.0
    for axis_at, parts in pieces:
        heights = jax.random.uniform(jax.random.fold_in(jax.random.fold_in(rng, 6), axis_at), (parts,), jnp.float32, low / len(pieces), top_value / len(pieces))
        loudness = loudness * jnp.repeat(jnp.exp(heights), dims[axis_at] // parts).reshape((-1,) + (1,) * (len(dims) - 1 - axis_at))
    return loudness


def gaussian(stream_key, dims, width, bound, split=(), kind=jnp.bfloat16):
    values = jax.random.normal(stream_key, dims, jnp.float32) * width
    if len(split) > 0:
        values = block_levels(stream_key, dims, split, -0.22, 0.18) * values
    return jnp.clip(values, min=-bound, max=bound).astype(kind)


def setup_inputs(seed: int = 0) -> dict:
    key_of = jax.random.split(jax.random.key(seed), 5)
    query_in = draw_query_in(jax.random.fold_in(key_of[4], 71), 0)
    key_in = draw_key_in(jax.random.fold_in(key_of[4], 71), 0)
    value_in = gaussian(key_of[2], (NT, NH, NW, HEADS * DH), 1.0, 6.0, ((0, 4), (1, 8), (2, 16)))
    cotangent = gaussian(key_of[3], (NT, NH, NW, HEADS * DH), 1.0, 6.0, ((0, 4), (1, 8), (2, 16)))
    return {"query_in": query_in, "key_in": key_in, "value_in": value_in, "cotangent": cotangent}


NEGATIVE = -1e+30

def rope_tables(time_pos, row_pos, col_pos):
    time_dims = DH // 8
    space_dims = (DH - time_dims) // 2
    slower = 256.0 ** (-jnp.arange(0, time_dims, 2, dtype=jnp.float32) / time_dims)
    faster = 256.0 ** (-jnp.arange(0, space_dims, 2, dtype=jnp.float32) / space_dims)
    angles = jnp.concatenate([time_pos[:, None] * slower, row_pos[:, None] * faster, col_pos[:, None] * faster], axis=1)
    return (jnp.cos(angles), jnp.sin(angles))

def rotate(flat_in, cosine, sine_tab, direction):
    row_total = flat_in.shape[0]
    paired = flat_in.reshape(row_total, HEADS, DH // 2, 2)
    real_part = paired[..., 0]
    imag_part = paired[..., 1]
    cos_rows = cosine[:, None, :]
    sin_rows = direction * sine_tab[:, None, :]
    turned = jnp.stack([real_part * cos_rows - imag_part * sin_rows, real_part * sin_rows + imag_part * cos_rows], axis=-1)
    return turned.reshape(row_total, HEADS * DH)

def reference(query_in, key_in, value_in, cotangent):
    frame_all, row_all, col_all, chan_count = query_in.shape
    cell_all = frame_all * row_all * col_all
    scale_factor = DH ** (-0.5)
    tiles_t = frame_all // TILE_T
    tiles_h = row_all // TILE_H
    tiles_w = col_all // TILE_W
    tile_count = tiles_t * tiles_h * tiles_w
    tile_cells = TILE_T * TILE_H * TILE_W
    per_frame = 9 * TILE_H * TILE_W
    shape_all = (frame_all, row_all, col_all)
    frame_grid = jnp.broadcast_to(jnp.arange(frame_all, dtype=jnp.int32)[:, None, None], shape_all).reshape(-1)
    row_grid = jnp.broadcast_to(jnp.arange(row_all, dtype=jnp.int32)[None, :, None], shape_all).reshape(-1)
    col_grid = jnp.broadcast_to(jnp.arange(col_all, dtype=jnp.int32)[None, None, :], shape_all).reshape(-1)
    cosine, sine_tab = rope_tables(frame_grid.astype(jnp.float32), row_grid.astype(jnp.float32), col_grid.astype(jnp.float32))
    query_rot = rotate(query_in.reshape(cell_all, chan_count).astype(jnp.float32), cosine, sine_tab, 1.0).astype(jnp.bfloat16).reshape(frame_all, row_all, col_all, chan_count)
    key_rot = rotate(key_in.reshape(cell_all, chan_count).astype(jnp.float32), cosine, sine_tab, 1.0).astype(jnp.bfloat16).reshape(frame_all, row_all, col_all, chan_count)

    def pad_space(grid_in):
        return jnp.pad(grid_in, ((0, 0), (TILE_H, TILE_H), (TILE_W, TILE_W), (0, 0)))

    def split_index(tile_idx):
        return (tile_idx // (tiles_h * tiles_w), tile_idx // tiles_w % tiles_h, tile_idx % tiles_w)

    def tile_of(grid_in, tile_idx):
        pos_t, pos_h, pos_w = split_index(tile_idx)
        block = lax.dynamic_slice(grid_in, (pos_t * TILE_T, pos_h * TILE_H, pos_w * TILE_W, jnp.int32(0)), (TILE_T, TILE_H, TILE_W, grid_in.shape[3]))
        return block.reshape(tile_cells, grid_in.shape[3])

    def window_of(grid_in, tile_idx):
        pos_t, pos_h, pos_w = split_index(tile_idx)
        block = lax.dynamic_slice(grid_in, (jnp.int32(0), pos_h * TILE_H, pos_w * TILE_W, jnp.int32(0)), (frame_all, 3 * TILE_H, 3 * TILE_W, grid_in.shape[3]))
        return block.reshape(frame_all * per_frame, grid_in.shape[3])

    def window_mask(tile_idx):
        pos_t, pos_h, pos_w = split_index(tile_idx)
        frame_ok = jnp.abs(pos_t - jnp.arange(frame_all, dtype=jnp.int32) // TILE_T) <= 1
        row_ids = pos_h * TILE_H - TILE_H + jnp.arange(3 * TILE_H, dtype=jnp.int32)
        col_ids = pos_w * TILE_W - TILE_W + jnp.arange(3 * TILE_W, dtype=jnp.int32)
        row_ok = (row_ids >= 0) & (row_ids < row_all)
        col_ok = (col_ids >= 0) & (col_ids < col_all)
        return (frame_ok[:, None, None] & row_ok[None, :, None] & col_ok[None, None, :]).reshape(-1)

    def heads_of(matrix):
        return matrix.reshape(matrix.shape[0], HEADS, DH).astype(jnp.float32)

    def ungrid(blocks):
        channels = blocks.shape[2]
        shaped = blocks.reshape(tiles_t, tiles_h, tiles_w, TILE_T, TILE_H, TILE_W, channels)
        return shaped.transpose(0, 3, 1, 4, 2, 5, 6).reshape(frame_all, row_all, col_all, channels)
    key_wide = pad_space(key_rot)
    value_wide = pad_space(value_in)
    tile_ids = jnp.arange(tile_count, dtype=jnp.int32)

    def forward_tile(tile_idx):
        query_tile = heads_of(tile_of(query_rot, tile_idx))
        key_window = heads_of(window_of(key_wide, tile_idx))
        value_window = heads_of(window_of(value_wide, tile_idx))
        visible = window_mask(tile_idx).reshape(frame_all, per_frame)
        scores = jnp.einsum('qhd,khd->hqk', query_tile, key_window) * scale_factor
        scores = scores.reshape(HEADS, tile_cells, frame_all, per_frame)
        frame_max = lax.optimization_barrier(jnp.max(jnp.where(visible, scores, NEGATIVE), axis=3))
        weights = jnp.where(visible, jnp.exp(scores - frame_max[..., None]), 0.0)
        frame_sum = lax.optimization_barrier(jnp.sum(weights, axis=3))
        frame_part = jnp.einsum('hqfk,fkhd->hqfd', weights.astype(jnp.bfloat16).astype(jnp.float32), value_window.reshape(frame_all, per_frame, HEADS, DH))
        highest = lax.optimization_barrier(jnp.max(frame_max, axis=2))
        factor = jnp.exp(frame_max - highest[..., None])
        denom = lax.optimization_barrier(jnp.sum(factor * frame_sum, axis=2))
        output = lax.optimization_barrier(jnp.sum(factor[..., None] * frame_part, axis=2)) / denom[..., None]
        return (jnp.transpose(output, (1, 0, 2)).reshape(tile_cells, chan_count), highest + jnp.log(denom))
    out_tiles, lse_tiles = lax.map(forward_tile, tile_ids)
    attended = ungrid(out_tiles).astype(jnp.bfloat16)
    lse_grid = ungrid(jnp.transpose(lse_tiles, (0, 2, 1)))
    delta_grid = lax.optimization_barrier(jnp.sum(cotangent.reshape(frame_all, row_all, col_all, HEADS, DH).astype(jnp.float32) * attended.reshape(frame_all, row_all, col_all, HEADS, DH).astype(jnp.float32), axis=4))

    def query_tile_grad(tile_idx):
        query_tile = heads_of(tile_of(query_rot, tile_idx))
        grad_tile = heads_of(tile_of(cotangent, tile_idx))
        lse_tile = tile_of(lse_grid, tile_idx)
        delta_tile = tile_of(delta_grid, tile_idx)
        key_window = heads_of(window_of(key_wide, tile_idx))
        value_window = heads_of(window_of(value_wide, tile_idx))
        visible = window_mask(tile_idx)
        scores = jnp.einsum('qhd,khd->hqk', query_tile, key_window) * scale_factor
        prob_rows = jnp.where(visible[None, None, :], jnp.exp(scores - lse_tile.T[:, :, None]), 0.0)
        prob_grad = jnp.einsum('qhd,khd->hqk', grad_tile, value_window)
        dscore = (prob_rows * (prob_grad - delta_tile.T[:, :, None])).astype(jnp.bfloat16).astype(jnp.float32)
        result = jnp.einsum('hqk,khd->qhd', dscore, key_window) * scale_factor
        return result.reshape(tile_cells, chan_count)
    query_wide = pad_space(query_rot)
    grad_wide = pad_space(cotangent)
    lse_wide = pad_space(lse_grid)
    delta_wide = pad_space(delta_grid)

    def key_tile_grad(tile_idx):
        key_tile = heads_of(tile_of(key_rot, tile_idx))
        value_tile = heads_of(tile_of(value_in, tile_idx))
        query_window = heads_of(window_of(query_wide, tile_idx))
        grad_window = heads_of(window_of(grad_wide, tile_idx))
        lse_window = window_of(lse_wide, tile_idx)
        delta_window = window_of(delta_wide, tile_idx)
        visible = window_mask(tile_idx)
        scores = jnp.einsum('khd,qhd->hkq', key_tile, query_window) * scale_factor
        prob_rows = jnp.where(visible[None, None, :], jnp.exp(scores - lse_window.T[:, None, :]), 0.0)
        value_grad = jnp.einsum('hkq,qhd->khd', prob_rows.astype(jnp.bfloat16).astype(jnp.float32), grad_window)
        prob_grad = jnp.einsum('khd,qhd->hkq', value_tile, grad_window)
        dscore = (prob_rows * (prob_grad - delta_window.T[:, None, :])).astype(jnp.bfloat16).astype(jnp.float32)
        key_grad = jnp.einsum('hkq,qhd->khd', dscore, query_window) * scale_factor
        return (key_grad.reshape(tile_cells, chan_count), value_grad.reshape(tile_cells, chan_count))
    dq_tiles = lax.map(query_tile_grad, tile_ids)
    dk_tiles, dv_tiles = lax.map(key_tile_grad, tile_ids)
    grad_query = rotate(ungrid(dq_tiles).reshape(cell_all, chan_count), cosine, sine_tab, -1.0).astype(jnp.bfloat16).reshape(frame_all, row_all, col_all, chan_count)
    grad_key = rotate(ungrid(dk_tiles).reshape(cell_all, chan_count), cosine, sine_tab, -1.0).astype(jnp.bfloat16).reshape(frame_all, row_all, col_all, chan_count)
    grad_value = ungrid(dv_tiles).astype(jnp.bfloat16)
    return (attended, grad_query, grad_key, grad_value)
```

```python
import functools

import jax
import jax.numpy as jnp
import numpy as np
from jax import lax
from jax.experimental import pallas as pl
from jax.experimental.pallas import tpu as pltpu
from jax.sharding import PartitionSpec as P

DH = 128
HEADS = 2
TILE = 8
FRAMES = 3
CELLS = FRAMES * TILE * TILE
CHAN = HEADS * DH
PAIR = 2 * CELLS
QUERIES = 4 * CELLS
SCALE = DH ** (-0.5)
EXP2_SCALE = SCALE * 1.4426950408889634
BIG = 1e30
POS = {2: 0, 1: 1, 3: 2, 0: 3}


def ahead(axis, step):
    size = lax.axis_size(axis)
    return lax.rem(lax.axis_index(axis) + (step + size), size)


def dot_nt(a, b):
    return lax.dot_general(a, b, (((1,), (1,)), ((), ())), preferred_element_type=jnp.float32)


def dot_tn(a, b):
    return lax.dot_general(a, b, (((0,), (0,)), ((), ())), preferred_element_type=jnp.float32)


def dot_nn(a, b):
    return lax.dot_general(a, b, (((1,), (0,)), ((), ())), preferred_element_type=jnp.float32)


def turn(block, cosine, sine, direction):
    lane = lax.broadcasted_iota(jnp.int32, (CELLS, DH), 1)
    nxt = pltpu.roll(block, DH - 1, 1)
    prv = pltpu.roll(block, 1, 1)
    swapped = jnp.where(lane % 2 == 0, -nxt, prv)
    return block * cosine + swapped * (direction * sine)


def head(idx):
    return pl.ds(idx * DH, DH)


def kernel(
    freq_ref, q_ref, k_ref, v_ref, g_ref,
    o_ref, dq_ref, dk_ref, dv_ref,
    kv, qs, gs, cos_tab, sin_tab, scores, probs, dsc, acc_t, dq_t, mrow,
    osend, orecv, lsend, lrecv, ssend, srecv, dqsend, dqrecv,
    part, hrecv, wsend, wrecv,
    halo_s, halo_r, ta_s, ta_r, o_s, o_r, l_s, l_r, st_s, st_r, dq_s, dq_r, h_s, h_r, w_s, w_r,
):
    t_pos, h_pos, w_pos = lax.axis_index("ta"), lax.axis_index("ha"), lax.axis_index("wa")
    h_size, w_size = lax.axis_size("ha"), lax.axis_size("wa")

    barrier = pltpu.get_barrier_semaphore()
    partners = [{"ha": ahead("ha", 1)}, {"ha": ahead("ha", -1)}, {"wa": ahead("wa", 1)}, {"wa": ahead("wa", -1)}]
    partners += [{"ta": ahead("ta", r)} for r in (1, 2, 3)]
    for partner in partners:
        pl.semaphore_signal(barrier, inc=1, device_id=partner, device_id_type=pl.DeviceIdType.MESH)

    lane = lax.broadcasted_iota(jnp.int32, (TILE, DH), 1)
    sub = lax.broadcasted_iota(jnp.int32, (TILE, DH), 0)
    in_time = lane < DH // 8
    in_row = lane < DH // 8 + (DH - DH // 8) // 2
    start = jnp.where(in_time, t_pos * FRAMES, jnp.where(in_row, h_pos * TILE, w_pos * TILE))
    angle = (start + sub).astype(jnp.float32) * freq_ref[...]
    for table, value in ((cos_tab, jnp.cos(angle)), (sin_tab, jnp.sin(angle))):
        for frame in range(FRAMES):
            for row in range(TILE):
                table[pl.ds((frame * TILE + row) * TILE, TILE), :] = jnp.where(
                    in_time,
                    jnp.broadcast_to(value[frame : frame + 1], (TILE, DH)),
                    jnp.where(in_row, jnp.broadcast_to(value[row : row + 1], (TILE, DH)), value),
                )
    own = pl.ds(POS[0] * CELLS, CELLS)
    for idx in range(HEADS):
        cosine, sine = cos_tab[...], sin_tab[...]
        kv[4, 0, :, head(idx)] = turn(k_ref[:, head(idx)].astype(jnp.float32), cosine, sine, 1.0).astype(jnp.bfloat16)
        qs[own, head(idx)] = turn(q_ref[:, head(idx)].astype(jnp.float32), cosine, sine, 1.0).astype(jnp.bfloat16)
    kv[4, 1] = v_ref[...]
    gs[own, :] = g_ref[...]

    pl.semaphore_wait(barrier, len(partners))

    def remote(src, dst, send, recv, device):
        return pltpu.make_async_remote_copy(
            src_ref=src, dst_ref=dst, send_sem=send, recv_sem=recv,
            device_id=device, device_id_type=pl.DeviceIdType.MESH,
        )

    def halo(kind, source, target, axis, step):
        return remote(
            kv.at[source, kind], kv.at[target, kind],
            halo_s.at[kind, target], halo_r.at[kind, target], {axis: ahead(axis, step)},
        )

    def spread(kind, r):
        buf = (qs, gs)[kind]
        return remote(
            buf.at[own], buf.at[pl.ds(POS[r] * CELLS, CELLS)],
            ta_s.at[kind, r - 1], ta_r.at[kind, r - 1], {"ta": ahead("ta", -r)},
        )

    sent = []

    def go(copy):
        copy.start()
        sent.append(copy)
        return copy

    for kind in (0, 1):
        w_copies = [go(halo(kind, 4, 3, "wa", 1)), go(halo(kind, 4, 5, "wa", -1))]
        go(halo(kind, 4, 1, "ha", 1))
        go(halo(kind, 4, 7, "ha", -1))
        if kind == 0:
            q_copies = [go(spread(0, r)) for r in (2, 1, 3)]
    for kind in (0, 1):
        halo(kind, 4, 3, "wa", 1).wait_recv()
        go(halo(kind, 3, 0, "ha", 1))
        go(halo(kind, 3, 6, "ha", -1))
        halo(kind, 4, 5, "wa", -1).wait_recv()
        go(halo(kind, 5, 2, "ha", 1))
        go(halo(kind, 5, 8, "ha", -1))
    g_copies = [go(spread(1, r)) for r in (2, 1, 3)]

    def hidden(slot):
        row = h_pos + slot // 3 - 1
        col = w_pos + slot % 3 - 1
        shown = (row >= 0) & (row < h_size) & (col >= 0) & (col < w_size)
        return jnp.where(shown, 0.0, BIG)

    for copy in q_copies:
        copy.wait_recv()
    for kind in (0, 1):
        for target in (1, 7, 0, 6, 2, 8):
            halo(kind, 4, target, "ha", 1).wait_recv()

    o_copies = []
    for group in range(2):
        queries = pl.ds(group * PAIR, PAIR)
        rows = []
        for idx in range(HEADS):

            def first(slot, best):
                tile = dot_nt(kv[slot, 0, :, head(idx)], qs[queries, head(idx)])
                scores[slot] = tile
                return jnp.maximum(best, jnp.max(tile.reshape(CELLS // 8, 8, PAIR), axis=0) - hidden(slot))

            best = lax.fori_loop(0, 9, first, jnp.full((8, PAIR), -BIG, jnp.float32))
            best = jnp.max(best, axis=0, keepdims=True)
            acc_t[...] = jnp.zeros_like(acc_t)

            def second(slot, total):
                tile = jnp.exp2((scores[slot] - (best + hidden(slot))) * EXP2_SCALE)
                tile16 = tile.astype(jnp.bfloat16)
                probs[idx, slot, :, queries] = tile16
                acc_t[...] += dot_tn(kv[slot, 1, :, head(idx)], tile16)
                return total + jnp.sum(tile.reshape(CELLS // 8, 8, PAIR), axis=0)

            total = lax.fori_loop(0, 9, second, jnp.zeros((8, PAIR), jnp.float32))
            total = jnp.sum(total, axis=0, keepdims=True)
            mrow[group, idx : idx + 1, :] = best * SCALE
            rows.append(best * SCALE + jnp.log(total))
            osend[queries, head(idx)] = jnp.transpose(acc_t[...] / total).astype(jnp.bfloat16)
        lsend[group] = jnp.concatenate(rows + [jnp.zeros((6, PAIR), jnp.float32)], axis=0)
        for r in ((2, 1), (3,))[group]:
            back = 4 - r
            dest = {"ta": ahead("ta", r)}
            o_copies.append(go(remote(
                osend.at[pl.ds(POS[r] * CELLS, CELLS)], orecv.at[back - 1],
                o_s.at[back - 1], o_r.at[back - 1], dest)))
            o_copies.append(go(remote(
                lsend.at[group], lrecv.at[back - 1], l_s.at[back - 1], l_r.at[back - 1], dest)))

    for copy in o_copies:
        copy.wait_recv()
    parts = [pltpu.roll(lsend[1], CELLS, 1), lrecv[0], lrecv[1], pltpu.roll(lrecv[2], CELLS, 1)]
    top = jnp.maximum(jnp.maximum(parts[0], parts[1]), jnp.maximum(parts[2], parts[3]))
    weights = [jnp.exp(piece - top) for piece in parts]
    denom = weights[0] + weights[1] + weights[2] + weights[3]
    lse = top + jnp.log(denom)
    wide = jnp.concatenate([piece / denom for piece in weights] + [jnp.zeros((96, PAIR), jnp.float32)], axis=0)
    columns = jnp.transpose(wide)[:CELLS]
    deltas = []
    for idx in range(HEADS):
        total = columns[:, idx : idx + 1] * osend[own, head(idx)].astype(jnp.float32)
        for src in range(3):
            at = 8 * (src + 1) + idx
            total = total + columns[:, at : at + 1] * orecv[src, :, head(idx)].astype(jnp.float32)
        rounded = total.astype(jnp.bfloat16)
        o_ref[:, head(idx)] = rounded
        product = rounded.astype(jnp.float32) * g_ref[:, head(idx)].astype(jnp.float32)
        product = jnp.concatenate([product, product], axis=0)
        deltas.append(jnp.sum(jnp.transpose(product), axis=0, keepdims=True))
    lane_pair = lax.broadcasted_iota(jnp.int32, (8, PAIR), 1)
    sub_pair = lax.broadcasted_iota(jnp.int32, (8, PAIR), 0)
    twice = jnp.where(lane_pair < CELLS, lse, pltpu.roll(lse, CELLS, 1))
    stats = jnp.where(
        sub_pair < 2, twice,
        jnp.where(sub_pair == 2, jnp.broadcast_to(deltas[0], (8, PAIR)), jnp.broadcast_to(deltas[1], (8, PAIR))),
    )
    ssend[...] = stats
    st_copies = []
    for r in (2, 1, 3):
        st_copies.append(go(remote(ssend, srecv.at[r - 1], st_s.at[r - 1], st_r.at[r - 1], {"ta": ahead("ta", -r)})))
    for copy in st_copies + g_copies:
        copy.wait_recv()

    low = lane_pair < CELLS
    stat_rows = [jnp.where(low, srecv[1], srecv[0]), jnp.where(low, srecv[2], ssend[...])]
    factor_rows = [jnp.exp(mrow[group] - stat_rows[group]) for group in range(2)]
    dq_t[...] = jnp.zeros_like(dq_t)

    def backward(slot):
        for idx in range(HEADS):
            keys, values = kv[slot, 0, :, head(idx)], kv[slot, 1, :, head(idx)]
            for group in range(2):
                queries = pl.ds(group * PAIR, PAIR)
                pgrad = dot_nt(values, gs[queries, head(idx)])
                prob = probs[idx, slot, :, queries].astype(jnp.float32) * factor_rows[group][idx : idx + 1]
                probs[idx, slot, :, queries] = prob.astype(jnp.bfloat16)
                dtile = (prob * (pgrad - stat_rows[group][2 + idx : 3 + idx])).astype(jnp.bfloat16)
                dsc[:, queries] = dtile
                dq_t[idx, :, queries] += dot_tn(keys, dtile)
            part[slot, 0, :, head(idx)] = (dot_nn(dsc[...], qs[:, head(idx)]) * SCALE).astype(jnp.bfloat16)
            part[slot, 1, :, head(idx)] = dot_nn(probs[idx, slot], gs[:, head(idx)]).astype(jnp.bfloat16)

    def to_row(step):
        side = step % 2
        col = (step // 2) * 2 % 3
        return remote(
            part.at[side * 6 + col], hrecv.at[col, 1 - side], h_s.at[col, 1 - side], h_r.at[col, 1 - side],
            {"ha": lax.rem(h_pos + 2 * side - 1 + h_size, h_size)},
        )

    def outer(step, carry):
        backward((step % 2) * 6 + (step // 2) * 2 % 3)
        to_row(step).start()
        return carry

    lax.fori_loop(0, 6, outer, 0)

    def inner(step, carry):
        backward(step)
        return carry

    lax.fori_loop(3, 6, inner, 0)

    for idx in range(HEADS):
        dqsend[:, head(idx)] = jnp.transpose(dq_t[idx] * SCALE).astype(jnp.bfloat16)
    dq_copies = []
    for r in (2, 1, 3):
        back = 4 - r
        dq_copies.append(go(remote(
            dqsend.at[pl.ds(POS[r] * CELLS, CELLS)], dqrecv.at[back - 1],
            dq_s.at[back - 1], dq_r.at[back - 1], {"ta": ahead("ta", r)})))

    w_copies = []
    for number, col in enumerate((0, 2)):
        for step in (2 * number, 2 * number + 1):
            to_row(step).wait_recv()
        for kind in range(2):
            wsend[number, kind] = (
                part[3 + col, kind].astype(jnp.float32)
                + hrecv[col, 0, kind].astype(jnp.float32)
                + hrecv[col, 1, kind].astype(jnp.float32)
            ).astype(jnp.bfloat16)
        w_copies.append(go(remote(
            wsend.at[number], wrecv.at[number], w_s.at[number], w_r.at[number], {"wa": ahead("wa", col - 1)})))
    for step in (4, 5):
        to_row(step).wait_recv()

    for copy in dq_copies:
        copy.wait_recv()
    for idx in range(HEADS):
        total = dqsend[own, head(idx)].astype(jnp.float32)
        for src in range(3):
            total = total + dqrecv[src, :, head(idx)].astype(jnp.float32)
        dq_ref[:, head(idx)] = turn(total, cos_tab[...], sin_tab[...], -1.0).astype(jnp.bfloat16)
    for copy in w_copies:
        copy.wait_recv()
    for kind, out in ((0, dk_ref), (1, dv_ref)):
        for idx in range(HEADS):
            total = part[4, kind, :, head(idx)].astype(jnp.float32)
            for side in range(2):
                total = total + hrecv[1, side, kind, :, head(idx)].astype(jnp.float32)
                total = total + wrecv[side, kind, :, head(idx)].astype(jnp.float32)
            if kind == 0:
                total = turn(total, cos_tab[...], sin_tab[...], -1.0)
            out[:, head(idx)] = total.astype(jnp.bfloat16)
    for step in range(6):
        to_row(step).wait_send()
    for copy in sent:
        copy.wait_send()


def shards(query_in, key_in, value_in, cotangent):
    time_dims = DH // 8
    space_dims = (DH - time_dims) // 2
    slower = 256.0 ** (-np.arange(0, time_dims, 2, dtype=np.float32) / np.float32(time_dims))
    faster = 256.0 ** (-np.arange(0, space_dims, 2, dtype=np.float32) / np.float32(space_dims))
    freq = np.repeat(np.concatenate([slower, faster, faster]).astype(np.float32), 2)
    freq = np.broadcast_to(freq[None, :], (TILE, DH))
    shape = query_in.shape
    bf16, f32 = jnp.bfloat16, jnp.float32
    block = (CELLS, CHAN)
    dma = pltpu.SemaphoreType.DMA
    outs = pl.pallas_call(
        kernel,
        out_shape=[jax.ShapeDtypeStruct(block, bf16)] * 4,
        in_specs=[pl.BlockSpec(memory_space=pltpu.VMEM)] * 5,
        out_specs=[pl.BlockSpec(memory_space=pltpu.VMEM)] * 4,
        scratch_shapes=[
            pltpu.VMEM((9, 2) + block, bf16),
            pltpu.VMEM((QUERIES, CHAN), bf16),
            pltpu.VMEM((QUERIES, CHAN), bf16),
            pltpu.VMEM((CELLS, DH), f32),
            pltpu.VMEM((CELLS, DH), f32),
            pltpu.VMEM((9, CELLS, PAIR), f32),
            pltpu.VMEM((HEADS, 9, CELLS, QUERIES), bf16),
            pltpu.VMEM((CELLS, QUERIES), bf16),
            pltpu.VMEM((DH, PAIR), f32),
            pltpu.VMEM((HEADS, DH, QUERIES), f32),
            pltpu.VMEM((2, 8, PAIR), f32),
            pltpu.VMEM((QUERIES, CHAN), bf16),
            pltpu.VMEM((3,) + block, bf16),
            pltpu.VMEM((2, 8, PAIR), f32),
            pltpu.VMEM((3, 8, PAIR), f32),
            pltpu.VMEM((8, PAIR), f32),
            pltpu.VMEM((3, 8, PAIR), f32),
            pltpu.VMEM((QUERIES, CHAN), bf16),
            pltpu.VMEM((3,) + block, bf16),
            pltpu.VMEM((9, 2) + block, bf16),
            pltpu.VMEM((3, 2, 2) + block, bf16),
            pltpu.VMEM((2, 2) + block, bf16),
            pltpu.VMEM((2, 2) + block, bf16),
            dma((2, 9)), dma((2, 9)), dma((2, 3)), dma((2, 3)),
            dma((3,)), dma((3,)), dma((3,)), dma((3,)), dma((3,)), dma((3,)), dma((3,)), dma((3,)),
            dma((3, 2)), dma((3, 2)), dma((2,)), dma((2,)),
        ],
        compiler_params=pltpu.CompilerParams(collective_id=0, has_side_effects=True),
    )(jnp.asarray(freq), *(arg.reshape(block) for arg in (query_in, key_in, value_in, cotangent)))
    return tuple(out.reshape(shape) for out in outs)


def solution(mesh):
    spec = P("ta", "ha", "wa", None)
    return jax.shard_map(shards, mesh=mesh, in_specs=(spec,) * 4, out_specs=(spec,) * 4, check_vma=False)
```

```python
import functools

import jax
import jax.numpy as jnp
from jax import lax
from jax.experimental import pallas as pl
from jax.experimental.pallas import tpu as pltpu
from jax.sharding import PartitionSpec as P

DH = 128
HEADS = 2
TILE = 8
FRAMES = 3
CELLS = FRAMES * TILE * TILE
CHAN = HEADS * DH
HALF = CELLS // 2
PAIR = 2 * CELLS
QUERIES = 4 * CELLS
SCALE = DH ** (-0.5)
EXP2_SCALE = SCALE * 1.4426950408889634
BIG = 1e30
POS = {2: 0, 1: 1, 3: 2, 0: 3}


def ahead(axis, step):
    size = lax.axis_size(axis)
    return lax.rem(lax.axis_index(axis) + (step + size), size)


def dot_nt(a, b):
    return lax.dot_general(a, b, (((1,), (1,)), ((), ())), preferred_element_type=jnp.float32)


def dot_tn(a, b):
    return lax.dot_general(a, b, (((0,), (0,)), ((), ())), preferred_element_type=jnp.float32)


def dot_nn(a, b):
    return lax.dot_general(a, b, (((1,), (0,)), ((), ())), preferred_element_type=jnp.float32)


def turn(block, cosine, sine, direction):
    lane = lax.broadcasted_iota(jnp.int32, (CELLS, DH), 1)
    nxt = pltpu.roll(block, DH - 1, 1)
    prv = pltpu.roll(block, 1, 1)
    swapped = jnp.where(lane % 2 == 0, -nxt, prv)
    return block * cosine + swapped * (direction * sine)


def head(idx):
    return pl.ds(idx * DH, DH)


def kernel(
    q_ref, k_ref, v_ref, g_ref,
    o_ref, dq_ref, dk_ref, dv_ref,
    kv, qs, gs, cos_tab, sin_tab, scores, probs, pgrads, dsc, acc_t, dq_t, mrow,
    osend, orecv, orelay, ssend, srecv, dqsend, dqrecv, dqrelay,
    part, hrecv, wsend, wrecv,
    halo_s, halo_r, ta_s, ta_r, o_s, o_r, st_s, st_r, dq_s, dq_r, h_s, h_r, w_s, w_r,
):
    t_pos, h_pos, w_pos = lax.axis_index("ta"), lax.axis_index("ha"), lax.axis_index("wa")
    h_size, w_size = lax.axis_size("ha"), lax.axis_size("wa")

    barrier = pltpu.get_barrier_semaphore()
    odd = lax.rem(w_pos, 2)
    pair_w = {"wa": w_pos + 1 - 2 * odd}
    far_w = {"wa": lax.rem(w_pos + 2 - 4 * odd + w_size, w_size)}
    near_w = {"wa": lax.rem(w_pos - 2 + 4 * odd + w_size, w_size)}
    partners = [{"ha": ahead("ha", 1)}, {"ha": ahead("ha", -1)}, pair_w, far_w, near_w]
    partners += [{"ta": ahead("ta", r)} for r in (1, 2, 3)]
    for partner in partners:
        pl.semaphore_signal(barrier, inc=1, device_id=partner, device_id_type=pl.DeviceIdType.MESH)

    lane = lax.broadcasted_iota(jnp.int32, (TILE, DH), 1)
    sub = lax.broadcasted_iota(jnp.int32, (TILE, DH), 0)
    in_time = lane < DH // 8
    in_row = lane < DH // 8 + (DH - DH // 8) // 2
    start = jnp.where(in_time, t_pos * FRAMES, jnp.where(in_row, h_pos * TILE, w_pos * TILE))
    pair = (lane // 2).astype(jnp.float32)
    time_dims, space_dims = DH // 8, (DH - DH // 8) // 2
    power = jnp.where(
        in_time, pair * (2.0 / time_dims),
        jnp.where(in_row, pair - time_dims // 2, pair - (time_dims + space_dims) // 2) * (2.0 / space_dims),
    )
    angle = (start + sub).astype(jnp.float32) * jnp.exp2(-8.0 * power)
    for table, value in ((cos_tab, jnp.cos(angle)), (sin_tab, jnp.sin(angle))):
        for frame in range(FRAMES):
            for row in range(TILE):
                table[pl.ds((frame * TILE + row) * TILE, TILE), :] = jnp.where(
                    in_time,
                    jnp.broadcast_to(value[frame : frame + 1], (TILE, DH)),
                    jnp.where(in_row, jnp.broadcast_to(value[row : row + 1], (TILE, DH)), value),
                )
    own = pl.ds(POS[0] * CELLS, CELLS)
    for idx in range(HEADS):
        cosine, sine = cos_tab[...], sin_tab[...]
        kv[4, 0, :, head(idx)] = turn(k_ref[:, head(idx)].astype(jnp.float32), cosine, sine, 1.0).astype(jnp.bfloat16)
        qs[own, head(idx)] = turn(q_ref[:, head(idx)].astype(jnp.float32), cosine, sine, 1.0).astype(jnp.bfloat16)
    kv[4, 1] = v_ref[...]
    gs[own, :] = g_ref[...]

    pl.semaphore_wait(barrier, len(partners))

    def remote(src, dst, send, recv, device):
        return pltpu.make_async_remote_copy(
            src_ref=src, dst_ref=dst, send_sem=send, recv_sem=recv,
            device_id=device, device_id_type=pl.DeviceIdType.MESH,
        )

    swap_slot, relay_slot = 5 - 2 * odd, 3 + 2 * odd

    def halo(kind, source, target, device):
        return remote(
            kv.at[source, kind], kv.at[target, kind], halo_s.at[kind, target], halo_r.at[kind, target], device,
        )

    def arrived(kind, target):
        halo(kind, 4, target, pair_w).wait_recv()

    def rows_of(r, part=None):
        if part is None:
            return pl.ds(POS[r] * CELLS, CELLS)
        return pl.ds(POS[r] * CELLS + part * HALF, HALF)

    def spread(kind, step):
        buf = (qs, gs)[kind]
        return remote(
            buf.at[own], buf.at[rows_of(4 - step if step > 0 else 1)],
            ta_s.at[kind, step], ta_r.at[kind, step], {"ta": ahead("ta", 1 if step == 1 else -1)},
        )

    def spread_on(kind, step):
        buf = (qs, gs)[kind]
        part = 0 if step == 1 else 1
        return remote(
            buf.at[rows_of(3 if step == 1 else 1, part)], buf.at[rows_of(2, part)],
            ta_s.at[kind, 2 + step], ta_r.at[kind, 2 + step], {"ta": ahead("ta", 1 if step == 1 else -1)},
        )

    sent = []

    def go(copy):
        copy.start()
        sent.append(copy)
        return copy

    def hidden(slot):
        row = h_pos + slot // 3 - 1
        col = w_pos + slot % 3 - 1
        shown = (row >= 0) & (row < h_size) & (col >= 0) & (col < w_size)
        return jnp.where(shown, 0.0, BIG)

    up_h, down_h = {"ha": ahead("ha", 1)}, {"ha": ahead("ha", -1)}

    def own_out(kind):
        go(halo(kind, 4, relay_slot, pair_w))
        go(halo(kind, 4, 1, up_h))
        go(halo(kind, 4, 7, down_h))
        for step in (1, 0):
            go(spread(kind, step))

    def swap_on(kind):
        arrived(kind, swap_slot)
        go(halo(kind, swap_slot, relay_slot, far_w))
        go(halo(kind, swap_slot, swap_slot - 3, up_h))
        go(halo(kind, swap_slot, swap_slot + 3, down_h))

    def relay_on(kind):
        arrived(kind, relay_slot)
        go(halo(kind, relay_slot, relay_slot - 3, up_h))
        go(halo(kind, relay_slot, relay_slot + 3, down_h))

    def chain_on(kind):
        for step in (1, 0):
            spread(kind, step).wait_recv()
            go(spread_on(kind, step))

    def all_in(kind):
        for target in (1, 7, 0, 6, 2, 8):
            arrived(kind, target)

    bests = {}

    def score_pass(group, idx):
        queries = pl.ds(group * PAIR, PAIR)

        def first(slot, best):
            tile = dot_nt(kv[slot, 0, :, head(idx)], qs[queries, head(idx)])
            scores[idx, slot] = tile
            return jnp.maximum(best, jnp.max(tile.reshape(CELLS // 8, 8, PAIR), axis=0) - hidden(slot))

        best = lax.fori_loop(0, 9, first, jnp.full((8, PAIR), -BIG, jnp.float32))
        bests[idx] = jnp.max(best, axis=0, keepdims=True)

    def prob_pass(group):
        queries = pl.ds(group * PAIR, PAIR)
        lses, deltas = [], []
        for idx in range(HEADS):
            best = bests[idx]

            def second(slot, sums):
                total, delta = sums
                tile = jnp.exp2((scores[idx, slot] - (best + hidden(slot))) * EXP2_SCALE)
                probs[idx, slot, :, queries] = tile.astype(jnp.bfloat16)
                pgrad = dot_nt(kv[slot, 1, :, head(idx)], gs[queries, head(idx)])
                pgrads[idx, slot, :, queries] = pgrad
                total = total + jnp.sum(tile.reshape(CELLS // 8, 8, PAIR), axis=0)
                delta = delta + jnp.sum((tile * pgrad).reshape(CELLS // 8, 8, PAIR), axis=0)
                return total, delta

            zero = jnp.zeros((8, PAIR), jnp.float32)
            total, delta = lax.fori_loop(0, 9, second, (zero, zero))
            total = jnp.sum(total, axis=0, keepdims=True)
            mrow[group, idx : idx + 1, :] = best * SCALE
            lses.append(best * SCALE + jnp.log(total))
            deltas.append(jnp.sum(delta, axis=0, keepdims=True) / total)
        ssend[group] = jnp.concatenate(lses + deltas + [jnp.zeros((4, PAIR), jnp.float32)], axis=0)
        for r in (2, 1, 3):
            go(stat_copy(group, r))

    def stat_copy(group, r):
        return remote(
            ssend.at[group], srecv.at[r - 1, group], st_s.at[group, r - 1], st_r.at[group, r - 1],
            {"ta": ahead("ta", -r)},
        )

    for kind in (0, 1):
        own_out(kind)
    swap_on(0)
    chain_on(0)
    relay_on(0)
    swap_on(1)
    all_in(0)
    score_pass(1, 0)
    relay_on(1)
    score_pass(1, 1)
    chain_on(1)
    all_in(1)
    prob_pass(1)
    for step in (1, 0):
        spread_on(0, step).wait_recv()
    score_pass(0, 0)
    score_pass(0, 1)
    for step in (1, 0):
        spread_on(1, step).wait_recv()
    prob_pass(0)

    acc_t[...] = jnp.zeros_like(acc_t)

    def third(slot, carry):
        for idx in range(HEADS):
            acc_t[idx] += dot_tn(kv[slot, 1, :, head(idx)], probs[idx, slot])
        return carry

    lax.fori_loop(0, 9, third, 0)

    for group in range(2):
        for r in (2, 1, 3):
            stat_copy(group, r).wait_recv()
    low = lax.broadcasted_iota(jnp.int32, (8, PAIR), 1) < CELLS
    factor_rows, delta_rows = [], []
    for group in range(2):
        mine = (2, 1) if group == 0 else (3, 0)
        pieces = []
        for src in range(4):
            halves = []
            for side in range(2):
                pos = POS[(mine[side] - src) % 4]
                rows = ssend[pos // 2] if src == 0 else srecv[src - 1, pos // 2]
                halves.append(rows if pos % 2 == side else pltpu.roll(rows, CELLS, 1))
            pieces.append(jnp.where(low, halves[0], halves[1]))
        top = jnp.maximum(jnp.maximum(pieces[0], pieces[1]), jnp.maximum(pieces[2], pieces[3]))[:HEADS]
        weights = [jnp.exp(piece[:HEADS] - top) for piece in pieces]
        denom = weights[0] + weights[1] + weights[2] + weights[3]
        delta = sum(weight * piece[HEADS : 2 * HEADS] for weight, piece in zip(weights, pieces)) / denom
        factor_rows.append(jnp.exp(mrow[group, :HEADS] - (top + jnp.log(denom))))
        delta_rows.append(delta)

    def ring(buf, relay, recv, send_sems, recv_sems):
        def half(step):
            part = 0 if step == 1 else 1
            return remote(
                buf.at[rows_of(2, part)], relay.at[part], send_sems.at[part], recv_sems.at[part],
                {"ta": ahead("ta", 1 if step == 1 else -1)},
            )

        def rest(step, part):
            r = 1 if step == 1 else 3
            return remote(
                buf.at[rows_of(r, part)], recv.at[step, pl.ds(part * HALF, HALF)],
                send_sems.at[2 + 2 * step + part], recv_sems.at[2 + 2 * step + part], {"ta": ahead("ta", r)},
            )

        def begin():
            for step in (1, 0):
                half(step).start()
            for step in (1, 0):
                rest(step, step).start()

        def merge():
            for step in (1, 0):
                part = 1 - step
                half(step).wait_recv()
                rows = rows_of(1 if step == 1 else 3, part)
                buf[rows, :] = (buf[rows, :].astype(jnp.float32) + relay[part].astype(jnp.float32)).astype(jnp.bfloat16)
            for step in (1, 0):
                rest(step, 1 - step).start()

        def finish():
            for step in (1, 0):
                for part in range(2):
                    rest(step, part).wait_recv()

        def leave():
            for step in (1, 0):
                half(step).wait_send()
                for part in range(2):
                    rest(step, part).wait_send()

        def total(idx):
            piece = buf[own, head(idx)].astype(jnp.float32)
            for src in range(2):
                piece = piece + recv[src, :, head(idx)].astype(jnp.float32)
            return piece

        return begin, merge, finish, leave, total

    o_ring = ring(osend, orelay, orecv, o_s, o_r)
    dq_ring = ring(dqsend, dqrelay, dqrecv, dq_s, dq_r)
    for idx in range(HEADS):
        for group in range(2):
            queries = pl.ds(group * PAIR, PAIR)
            weighted = acc_t[idx, :, queries] * factor_rows[group][idx : idx + 1]
            osend[queries, head(idx)] = jnp.transpose(weighted).astype(jnp.bfloat16)
    o_ring[0]()
    dq_t[...] = jnp.zeros_like(dq_t)

    def backward(slot):
        for idx in range(HEADS):
            keys = kv[slot, 0, :, head(idx)]
            for group in range(2):
                queries = pl.ds(group * PAIR, PAIR)
                prob = probs[idx, slot, :, queries].astype(jnp.float32) * factor_rows[group][idx : idx + 1]
                probs[idx, slot, :, queries] = prob.astype(jnp.bfloat16)
                dtile = prob * (pgrads[idx, slot, :, queries] - delta_rows[group][idx : idx + 1])
                dsc[:, queries] = dtile.astype(jnp.bfloat16)
            dq_t[idx] += dot_tn(keys, dsc[...])
            part[slot, 0, :, head(idx)] = (dot_nn(dsc[...], qs[:, head(idx)]) * SCALE).astype(jnp.bfloat16)
            part[slot, 1, :, head(idx)] = dot_nn(probs[idx, slot], gs[:, head(idx)]).astype(jnp.bfloat16)

    def column(turn_idx):
        return jnp.where(turn_idx == 0, 2 * odd, jnp.where(turn_idx == 1, 2 - 2 * odd, 1))

    def to_row(turn_idx, side):
        return remote(
            part.at[side * 6 + column(turn_idx)], hrecv.at[turn_idx, 1 - side],
            h_s.at[turn_idx, 1 - side], h_r.at[turn_idx, 1 - side],
            {"ha": lax.rem(h_pos + 2 * side - 1 + h_size, h_size)},
        )

    def along_y():
        return remote(wsend.at[0], wrecv.at[0], w_s.at[0], w_r.at[0], near_w)

    def along_z():
        return remote(wsend.at[1], wrecv.at[1], w_s.at[1], w_r.at[1], pair_w)

    def gather_rows(turn_idx, kind):
        return (
            part[3 + column(turn_idx), kind].astype(jnp.float32)
            + hrecv[turn_idx, 0, kind].astype(jnp.float32)
            + hrecv[turn_idx, 1, kind].astype(jnp.float32)
        )

    def outer(step, carry):
        turn_idx, place = step // 3, step % 3
        backward(place * 2 % 3 * 3 + column(turn_idx))

        @pl.when(place < 2)
        def _():
            to_row(turn_idx, place).start()

        @pl.when(step == 2)
        def _():
            o_ring[1]()

        @pl.when(step == 3)
        def _():
            for side in range(2):
                to_row(0, side).wait_recv()
            for kind in range(2):
                wsend[0, kind] = gather_rows(0, kind).astype(jnp.bfloat16)
            along_y().start()

        return carry

    lax.fori_loop(0, 9, outer, 0)

    for idx in range(HEADS):
        dqsend[:, head(idx)] = jnp.transpose(dq_t[idx] * SCALE).astype(jnp.bfloat16)

    dq_ring[0]()

    for side in range(2):
        to_row(1, side).wait_recv()
    along_y().wait_recv()
    for kind in range(2):
        wsend[1, kind] = (gather_rows(1, kind) + wrecv[0, kind].astype(jnp.float32)).astype(jnp.bfloat16)
    along_z().start()
    dq_ring[1]()

    o_ring[2]()
    for idx in range(HEADS):
        o_ref[:, head(idx)] = o_ring[4](idx).astype(jnp.bfloat16)
    for side in range(2):
        to_row(2, side).wait_recv()
    dq_ring[2]()
    for idx in range(HEADS):
        dq_ref[:, head(idx)] = turn(dq_ring[4](idx), cos_tab[...], sin_tab[...], -1.0).astype(jnp.bfloat16)
    along_z().wait_recv()
    for kind, out in ((0, dk_ref), (1, dv_ref)):
        for idx in range(HEADS):
            total = part[4, kind, :, head(idx)].astype(jnp.float32)
            for side in range(2):
                total = total + hrecv[2, side, kind, :, head(idx)].astype(jnp.float32)
            total = total + wrecv[1, kind, :, head(idx)].astype(jnp.float32)
            if kind == 0:
                total = turn(total, cos_tab[...], sin_tab[...], -1.0)
            out[:, head(idx)] = total.astype(jnp.bfloat16)
    for turn_idx in range(3):
        for side in range(2):
            to_row(turn_idx, side).wait_send()
    along_y().wait_send()
    along_z().wait_send()
    o_ring[3]()
    dq_ring[3]()
    for copy in sent:
        copy.wait_send()


def shards(query_in, key_in, value_in, cotangent):
    shape = query_in.shape
    bf16, f32 = jnp.bfloat16, jnp.float32
    block = (CELLS, CHAN)
    dma = pltpu.SemaphoreType.DMA
    outs = pl.pallas_call(
        kernel,
        out_shape=[jax.ShapeDtypeStruct(block, bf16)] * 4,
        in_specs=[pl.BlockSpec(memory_space=pltpu.VMEM)] * 4,
        out_specs=[pl.BlockSpec(memory_space=pltpu.VMEM)] * 4,
        scratch_shapes=[
            pltpu.VMEM((9, 2) + block, bf16),
            pltpu.VMEM((QUERIES, CHAN), bf16),
            pltpu.VMEM((QUERIES, CHAN), bf16),
            pltpu.VMEM((CELLS, DH), f32),
            pltpu.VMEM((CELLS, DH), f32),
            pltpu.VMEM((HEADS, 9, CELLS, PAIR), f32),
            pltpu.VMEM((HEADS, 9, CELLS, QUERIES), bf16),
            pltpu.VMEM((HEADS, 9, CELLS, QUERIES), f32),
            pltpu.VMEM((CELLS, QUERIES), bf16),
            pltpu.VMEM((HEADS, DH, QUERIES), f32),
            pltpu.VMEM((HEADS, DH, QUERIES), f32),
            pltpu.VMEM((2, 8, PAIR), f32),
            pltpu.VMEM((QUERIES, CHAN), bf16),
            pltpu.VMEM((2,) + block, bf16),
            pltpu.VMEM((2, HALF, CHAN), bf16),
            pltpu.VMEM((2, 8, PAIR), f32),
            pltpu.VMEM((3, 2, 8, PAIR), f32),
            pltpu.VMEM((QUERIES, CHAN), bf16),
            pltpu.VMEM((2,) + block, bf16),
            pltpu.VMEM((2, HALF, CHAN), bf16),
            pltpu.VMEM((9, 2) + block, bf16),
            pltpu.VMEM((3, 2, 2) + block, bf16),
            pltpu.VMEM((2, 2) + block, bf16),
            pltpu.VMEM((2, 2) + block, bf16),
            dma((2, 9)), dma((2, 9)), dma((2, 4)), dma((2, 4)),
            dma((6,)), dma((6,)), dma((2, 3)), dma((2, 3)), dma((6,)), dma((6,)),
            dma((3, 2)), dma((3, 2)), dma((2,)), dma((2,)),
        ],
        compiler_params=pltpu.CompilerParams(collective_id=0, has_side_effects=True),
    )(*(arg.reshape(block) for arg in (query_in, key_in, value_in, cotangent)))
    return tuple(out.reshape(shape) for out in outs)


def solution(mesh):
    spec = P("ta", "ha", "wa", None)
    return jax.shard_map(shards, mesh=mesh, in_specs=(spec,) * 4, out_specs=(spec,) * 4, check_vma=False)
```
